32 devices in a mesh: groups: 2 (over y), seq: 4 (over x, core), sub: 4 (over z).
Axes of the slice: x: 2, y: 2, z: 4, core: 2. Of those that a mesh axis runs over, the one named last changes fastest.
Arguments:
- queries: bfloat16 [16384, 1024], P(('groups', 'seq', 'sub')), parts along dimension 0, may hold values from -6 to 6
- key_vectors: bfloat16 [16384, 1024], P(('groups', 'seq', 'sub')), parts along dimension 0, may hold values from -6 to 6
- value_vectors: bfloat16 [16384, 1024], P(('groups', 'seq', 'sub')), parts along dimension 0, may hold values from -16 to 16
- cotangent: bfloat16 [16384, 1024], P(('groups', 'seq', 'sub')), parts along dimension 0, may hold values from -6 to 6
- norm_gain: float32 [1024], replicated, may hold values from 0.1 to 1.9
Outputs:
- attended_out: bfloat16 [16384, 1024], P(('groups', 'seq', 'sub')), parts along dimension 0
- query_grad: bfloat16 [16384, 1024], P(('groups', 'seq', 'sub')), parts along dimension 0
- key_grad: bfloat16 [16384, 1024], P(('groups', 'seq', 'sub')), parts along dimension 0
- value_grad: bfloat16 [16384, 1024], P(('groups', 'seq', 'sub')), parts along dimension 0
The draws below stay inside these ranges and needn't reach their ends.
There are 2 independent parts, one for each index of `groups`. The reference program is written for one: setup_inputs(seed, part) draws one part's arguments, and reference() takes and returns one part's arrays. A program takes and returns all parts, laid end to end along the dimension named above; an argument that names none is the same for every part. Nothing has to cross between parts.
All inputs are finite; a program needn't handle non-finite values.
Results may differ from the reference program's by a relative error of at most 0.0058.
Values sent between devices are 32-bit elements; how exact they have to be, the bound alone decides.
A program may use at most 192 MiB of HBM per device.

```python
from functools import partial
import jax
import jax.numpy as jnp
from jax import lax

H = 8
DH = 128
D = 1024
BLK = 512
TOKENS = 8192


def draw_value_vectors(key, part):
    scale_key, noise_key = jax.random.split(key, 2)
    column_scale = jnp.exp(jax.random.uniform(scale_key, (H * DH,), jnp.float32, -1.2, 1.2))
    noise_part = jnp.clip(jax.random.normal(noise_key, (TOKENS, H * DH), jnp.float32), -4.0, 4.0)
    return (noise_part * column_scale).astype(jnp.bfloat16)


def shard_levels(own_key, dims, cuts, smallest, high):
    loudness, own = 1.0, jax.random.fold_in(own_key, 6)
    for dim, shards_of in cuts:
        draws = jnp.exp(jax.random.uniform(jax.random.fold_in(own, dim), (shards_of,), jnp.float32, smallest / len(cuts), high / len(cuts)))
        loudness = loudness * jnp.repeat(draws, dims[dim] // shards_of).reshape([-1 if axis == dim else 1 for axis in range(len(dims))])
    return loudness


def normal_values(rng, shape, width, most, cuts=(), held_as=jnp.bfloat16):
    values = jax.random.normal(rng, shape, jnp.float32) * width
    if len(cuts) > 0:
        values = shard_levels(rng, shape, cuts, -0.22, 0.18) * values
    return jnp.clip(values, min=-most, max=most).astype(held_as)


def setup_inputs(seed: int = 0, part: int = 0) -> dict:
    key_of = jax.random.split(jax.random.key(seed), 6)
    part_splits = jax.random.split(jax.random.fold_in(key_of[5], part), 6)
    return {
        "queries": normal_values(part_splits[0], (TOKENS, D), 1.0, 6.0, ((0, 16),)),
        "key_vectors": normal_values(part_splits[1], (TOKENS, D), 1.0, 6.0, ((0, 16),)),
        "value_vectors": draw_value_vectors(jax.random.fold_in(jax.random.fold_in(key_of[5], part), 71), part),
        "cotangent": normal_values(part_splits[3], (TOKENS, D), 1.0, 6.0, ((0, 16),)),
        "norm_gain": jnp.clip(1.0 + 0.18 * jax.random.normal(key_of[4], (D,), jnp.float32), 0.1, 1.9),
    }


def normalize(attended, gain_heads):
    inverse = lax.rsqrt(lax.optimization_barrier(jnp.mean(attended * attended, axis=-1, keepdims=True)) + 1e-05)
    return attended * inverse * gain_heads

def as_float(array):
    return array.astype(jnp.float32)

def reference(queries, key_vectors, value_vectors, cotangent, norm_gain):
    num_blocks = TOKENS // BLK
    shape_blocks = (num_blocks, BLK, H, DH)
    query_blocks = queries.reshape(shape_blocks)
    key_blocks = key_vectors.reshape(shape_blocks)
    value_blocks = value_vectors.reshape(shape_blocks)
    causal = (jnp.arange(BLK)[:, None] >= jnp.arange(BLK)[None, :])[None]
    gain_heads = norm_gain.reshape(H, DH)
    initial = jnp.zeros((H, DH, DH), jnp.float32)

    def forward_step(state, inputs):
        query_block, key_block, value_block = inputs
        scores = jnp.einsum('shd,thd->hst', as_float(query_block), as_float(key_block))
        scores = jnp.where(causal, scores, 0.0).astype(jnp.bfloat16)
        state_low = state.astype(jnp.bfloat16)
        attended = jnp.einsum('hst,thd->shd', as_float(scores), as_float(value_block))
        attended = attended + jnp.einsum('shd,hde->she', as_float(query_block), as_float(state_low))
        update = jnp.einsum('thd,the->hde', as_float(key_block), as_float(value_block))
        return (state + update, (attended, state_low))
    unused, (attended, states_low) = lax.scan(forward_step, initial, (query_blocks, key_blocks, value_blocks))
    normed, pullback = jax.vjp(partial(normalize, gain_heads=gain_heads), attended)
    attended_out = normed.astype(jnp.bfloat16).reshape(TOKENS, H * DH)
    grad_blocks = pullback(as_float(cotangent).reshape(shape_blocks))[0].astype(jnp.bfloat16)

    def backward_step(carry_state, inputs):
        query_block, key_block, value_block, grad_block, state_low = inputs
        after_low = carry_state.astype(jnp.bfloat16)
        scores = jnp.einsum('shd,thd->hst', as_float(query_block), as_float(key_block))
        scores = jnp.where(causal, scores, 0.0).astype(jnp.bfloat16)
        grad_scores = jnp.einsum('she,the->hst', as_float(grad_block), as_float(value_block))
        grad_scores = jnp.where(causal, grad_scores, 0.0).astype(jnp.bfloat16)
        query_grad = jnp.einsum('hst,thd->shd', as_float(grad_scores), as_float(key_block))
        query_grad = query_grad + jnp.einsum('she,hde->shd', as_float(grad_block), as_float(state_low))
        key_grad = jnp.einsum('hst,shd->thd', as_float(grad_scores), as_float(query_block))
        key_grad = key_grad + jnp.einsum('the,hde->thd', as_float(value_block), as_float(after_low))
        value_grad = jnp.einsum('hst,she->the', as_float(scores), as_float(grad_block))
        value_grad = value_grad + jnp.einsum('thd,hde->the', as_float(key_block), as_float(after_low))
        update = jnp.einsum('shd,she->hde', as_float(query_block), as_float(grad_block))
        return (carry_state + update, (query_grad.astype(jnp.bfloat16), key_grad.astype(jnp.bfloat16), value_grad.astype(jnp.bfloat16)))
    unused_too, (query_grad, key_grad, value_grad) = lax.scan(backward_step, initial, (query_blocks, key_blocks, value_blocks, grad_blocks, states_low), reverse=True)
    return (attended_out, query_grad.reshape(TOKENS, H * DH), key_grad.reshape(TOKENS, H * DH), value_grad.reshape(TOKENS, H * DH))
```

```python
import functools

import jax
import jax.numpy as jnp
from jax import lax
from jax.experimental import pallas as pl
from jax.experimental.pallas import tpu as pltpu
from jax.sharding import PartitionSpec as P

H = 8
DH = 128
BLK = 512
MESH = pl.DeviceIdType.MESH


def mm(a, b, ca, cb):
    return lax.dot_general(a, b, (((ca,), (cb,)), ((), ())), preferred_element_type=jnp.float32)


def kernel(
    n_seq, n_sub, q_ref, k_ref, v_ref, c_ref, gain_ref,
    out_ref, dq_ref, dk_ref, dv_ref,
    part, pieces, sums, enter, back_part, back_pieces, back_sums, back_enter,
    scores, attended, grad, dk_part, dv_part,
    send_sems, recv_sems,
):
    count = n_seq * n_sub
    rows = H * DH // count
    me = lax.axis_index("seq") * n_sub + lax.axis_index("sub")

    def where(peer):
        return {"seq": peer // n_sub, "sub": lax.rem(peer, n_sub)}

    def other(step):
        return lax.rem(me + step, count)

    def head(h):
        return pl.ds(pl.multiple_of(h * DH, DH), DH)

    def chunk(owner):
        return pl.ds(pl.multiple_of(owner * rows, rows), rows)

    barrier = pltpu.get_barrier_semaphore()

    @pl.loop(1, count)
    def _(step):
        pl.semaphore_signal(barrier, inc=1, device_id=where(other(step)), device_id_type=MESH)

    def drain(buffer, sem):
        whole = buffer.at[pl.ds(0, count - 1)]
        pltpu.make_async_copy(whole, whole, sem).wait()

    def spread(source, landing, phase):
        @pl.loop(1, count)
        def _(step):
            peer = other(step)
            pltpu.make_async_remote_copy(
                src_ref=source.at[chunk(peer)],
                dst_ref=landing.at[me],
                send_sem=send_sems.at[phase],
                recv_sem=recv_sems.at[phase],
                device_id=where(peer),
                device_id_type=MESH,
            ).start()

    def give_back(landing, totals, result, phase, reverse):
        def add_up(turn, total):
            peer = count - 1 - turn if reverse else turn
            totals[peer] = total
            return total + landing[peer]

        lax.fori_loop(0, count, add_up, jnp.zeros((rows, DH), jnp.float32))

        @pl.loop(1, count)
        def _(step):
            peer = other(step)
            pltpu.make_async_remote_copy(
                src_ref=totals.at[peer],
                dst_ref=result.at[chunk(me)],
                send_sem=send_sems.at[phase],
                recv_sem=recv_sems.at[phase],
                device_id=where(peer),
                device_id_type=MESH,
            ).start()

        result[chunk(me), :] = totals[me]

    @pl.loop(0, H)
    def _(h):
        part[head(h), :] = mm(k_ref[:, head(h)], v_ref[:, head(h)], 0, 0)

    pieces[me] = part[chunk(me), :]
    pl.semaphore_wait(barrier, count - 1)
    spread(part, pieces, 0)

    causal = lax.broadcasted_iota(jnp.int32, (BLK, BLK), 0) >= lax.broadcasted_iota(
        jnp.int32, (BLK, BLK), 1
    )

    @pl.loop(0, H)
    def _(h):
        s = mm(q_ref[:, head(h)], k_ref[:, head(h)], 1, 1)
        scores[h] = jnp.where(causal, s, 0.0).astype(jnp.bfloat16)

    drain(pieces, recv_sems.at[0])
    give_back(pieces, sums, enter, 1, False)

    @pl.loop(0, H)
    def _(h):
        attended[:, head(h)] = mm(scores[h], v_ref[:, head(h)], 1, 0)

    drain(pieces, recv_sems.at[1])

    @pl.loop(0, H)
    def _(h):
        q = q_ref[:, head(h)]
        att = attended[:, head(h)] + mm(q, enter[head(h), :].astype(jnp.bfloat16), 1, 0)
        inverse = lax.rsqrt(jnp.mean(att * att, axis=-1, keepdims=True) + 1e-05)
        gain = gain_ref[:, head(h)]
        out_ref[:, head(h)] = (att * inverse * gain).astype(jnp.bfloat16)
        scaled = c_ref[:, head(h)].astype(jnp.float32) * gain
        along = jnp.mean(scaled * att, axis=-1, keepdims=True) * inverse * inverse
        g = (inverse * (scaled - att * along)).astype(jnp.bfloat16)
        grad[:, head(h)] = g
        back_part[head(h), :] = mm(q, g, 0, 0)

    back_pieces[me] = back_part[chunk(me), :]
    spread(back_part, back_pieces, 2)

    @pl.loop(0, H)
    def _(h):
        g = grad[:, head(h)]
        s = mm(g, v_ref[:, head(h)], 1, 1)
        s = jnp.where(causal, s, 0.0).astype(jnp.bfloat16)
        dq = mm(s, k_ref[:, head(h)], 1, 0)
        dq = dq + mm(g, enter[head(h), :].astype(jnp.bfloat16), 1, 1)
        dq_ref[:, head(h)] = dq.astype(jnp.bfloat16)
        dk_part[:, head(h)] = mm(s, q_ref[:, head(h)], 0, 0)

    drain(back_pieces, recv_sems.at[2])
    give_back(back_pieces, back_sums, back_enter, 3, True)

    @pl.loop(0, H)
    def _(h):
        dv_part[:, head(h)] = mm(scores[h], grad[:, head(h)], 0, 0)

    drain(back_pieces, recv_sems.at[3])

    @pl.loop(0, H)
    def _(h):
        after = back_enter[head(h), :].astype(jnp.bfloat16)
        dk = dk_part[:, head(h)] + mm(v_ref[:, head(h)], after, 1, 1)
        dk_ref[:, head(h)] = dk.astype(jnp.bfloat16)
        dv = dv_part[:, head(h)] + mm(k_ref[:, head(h)], after, 1, 0)
        dv_ref[:, head(h)] = dv.astype(jnp.bfloat16)

    for phase in range(4):
        drain(pieces, send_sems.at[phase])


def local(n_seq, n_sub, queries, key_vectors, value_vectors, cotangent, norm_gain):
    count = n_seq * n_sub
    rows = H * DH // count
    width = H * DH
    vmem = pl.BlockSpec(memory_space=pltpu.VMEM)
    state = pltpu.VMEM((width, DH), jnp.float32)
    split = pltpu.VMEM((count, rows, DH), jnp.float32)
    wide = pltpu.VMEM((BLK, width), jnp.float32)
    return pl.pallas_call(
        functools.partial(kernel, n_seq, n_sub),
        out_shape=[jax.ShapeDtypeStruct((BLK, width), jnp.bfloat16)] * 4,
        in_specs=[vmem] * 5,
        out_specs=[vmem] * 4,
        scratch_shapes=[
            state, split, split, state, state, split, split, state,
            pltpu.VMEM((H, BLK, BLK), jnp.bfloat16),
            wide,
            pltpu.VMEM((BLK, width), jnp.bfloat16),
            wide,
            wide,
            pltpu.SemaphoreType.DMA((4,)),
            pltpu.SemaphoreType.DMA((4,)),
        ],
        compiler_params=pltpu.CompilerParams(
            collective_id=0, has_side_effects=True, vmem_limit_bytes=48 << 20
        ),
    )(queries, key_vectors, value_vectors, cotangent, norm_gain.reshape(1, width))


def solution(mesh):
    rows = P(("groups", "seq", "sub"), None)
    return jax.shard_map(
        functools.partial(local, mesh.shape["seq"], mesh.shape["sub"]),
        mesh=mesh,
        in_specs=(rows, rows, rows, rows, P()),
        out_specs=(rows, rows, rows, rows),
        check_vma=False,
    )
```

```python
import functools

import jax
import jax.numpy as jnp
from jax import lax
from jax.experimental import pallas as pl
from jax.experimental.pallas import tpu as pltpu
from jax.sharding import PartitionSpec as P

H = 8
DH = 128
BLK = 512
SUB_SKEW = 2
SEQ_SKEW = 1
MESH = pl.DeviceIdType.MESH


def mm(a, b, ca, cb):
    return lax.dot_general(a, b, (((ca,), (cb,)), ((), ())), preferred_element_type=jnp.float32)


def kernel(
    n_seq, n_sub, q_ref, k_ref, v_ref, c_ref, gain_ref,
    out_ref, dq_ref, dk_ref, dv_ref,
    own, up_in, up_out, down_in, down_out, seq_in, seq_out,
    scores, attended, grad, dk_part, dv_part,
    send_sems, recv_sems,
):
    row = lax.axis_index("seq")
    place = lax.axis_index("sub")
    has_prev, has_next = place > 0, place < n_sub - 1
    has_prev_row, has_next_row = row > 0, row < n_seq - 1
    depth = SUB_SKEW * (n_sub - 1) + SEQ_SKEW * (n_seq - 1)

    def head(h):
        return pl.ds(pl.multiple_of(h * DH, DH), DH)

    def at_sub(step):
        return {"sub": place + step}

    def at_seq(step):
        return {"seq": row + step}

    barrier = pltpu.get_barrier_semaphore()
    neighbours = (
        (has_prev, at_sub(-1)), (has_next, at_sub(1)),
        (has_prev_row, at_seq(-1)), (has_next_row, at_seq(1)),
    )
    for exists, device in neighbours:
        @pl.when(exists)
        def _(device=device):
            pl.semaphore_signal(barrier, inc=1, device_id=device, device_id_type=MESH)

    first_row = (jnp.logical_not(has_prev_row), jnp.logical_not(has_next_row))
    for scan in range(2):
        for empty, buffer in (
            (jnp.logical_not(has_prev), up_in),
            (jnp.logical_not(has_next), down_in),
            (first_row[scan], seq_in),
        ):
            @pl.when(empty)
            def _(buffer=buffer, scan=scan):
                buffer[scan] = jnp.zeros((H, DH, DH), jnp.float32)

    def hop(source, landing, scan, kind, h, device):
        return pltpu.make_async_remote_copy(
            src_ref=source.at[scan, h],
            dst_ref=landing.at[scan, h],
            send_sem=send_sems.at[scan, kind],
            recv_sem=recv_sems.at[scan, kind, h],
            device_id=device,
            device_id_type=MESH,
        )

    def in_turn(h, body):
        @pl.when(jnp.logical_and(h >= 0, h < H))
        def _():
            body(h)

    def link(landing, source, scan, kind, h, arrives, leaves, step, value):
        @pl.when(arrives)
        def _():
            hop(source, landing, scan, kind, h, step).wait_recv()

        source[scan, h] = value()

        @pl.when(leaves)
        def _():
            hop(source, landing, scan, kind, h, step).start()

    def up(scan):
        def body(h):
            link(up_in, up_out, scan, 0, h, has_prev, has_next, at_sub(1),
                 lambda: up_in[scan, h] + own[scan, h])
        return body

    def down(scan):
        def body(h):
            link(down_in, down_out, scan, 1, h, has_next, has_prev, at_sub(-1),
                 lambda: down_in[scan, h] + own[scan, h])
        return body

    def along_seq(scan):
        arrives, leaves, step = (
            (has_prev_row, has_next_row, at_seq(1)),
            (has_next_row, has_prev_row, at_seq(-1)),
        )[scan]

        def body(h):
            link(seq_in, seq_out, scan, 2, h, arrives, leaves, step,
                 lambda: seq_in[scan, h] + (up_out[scan, h] + down_in[scan, h]))
        return body

    def entering(scan, h):
        within = (up_in, down_in)[scan]
        return (seq_in[scan, h] + within[scan, h]).astype(jnp.bfloat16)

    def key_value_state(h):
        own[0, h] = mm(k_ref[:, head(h)], v_ref[:, head(h)], 0, 0)

    causal = lax.broadcasted_iota(jnp.int32, (BLK, BLK), 0) >= lax.broadcasted_iota(
        jnp.int32, (BLK, BLK), 1
    )

    def within_block(h):
        s = mm(q_ref[:, head(h)], k_ref[:, head(h)], 1, 1)
        s = jnp.where(causal, s, 0.0).astype(jnp.bfloat16)
        scores[h] = s
        attended[:, head(h)] = mm(s, v_ref[:, head(h)], 1, 0)

    def norm_and_pullback(h):
        q = q_ref[:, head(h)]
        att = attended[:, head(h)] + mm(q, entering(0, h), 1, 0)
        inverse = lax.rsqrt(jnp.mean(att * att, axis=-1, keepdims=True) + 1e-05)
        gain = gain_ref[:, head(h)]
        out_ref[:, head(h)] = (att * inverse * gain).astype(jnp.bfloat16)
        scaled = c_ref[:, head(h)].astype(jnp.float32) * gain
        along = jnp.mean(scaled * att, axis=-1, keepdims=True) * inverse * inverse
        g = (inverse * (scaled - att * along)).astype(jnp.bfloat16)
        grad[:, head(h)] = g
        own[1, h] = mm(q, g, 0, 0)

    def gradients_within(h):
        g = grad[:, head(h)]
        s = mm(g, v_ref[:, head(h)], 1, 1)
        s = jnp.where(causal, s, 0.0).astype(jnp.bfloat16)
        dq = mm(s, k_ref[:, head(h)], 1, 0) + mm(g, entering(0, h), 1, 1)
        dq_ref[:, head(h)] = dq.astype(jnp.bfloat16)
        dk_part[:, head(h)] = mm(s, q_ref[:, head(h)], 0, 0)
        dv_part[:, head(h)] = mm(scores[h], g, 0, 0)

    def finish(h):
        after = entering(1, h)
        dk = dk_part[:, head(h)] + mm(v_ref[:, head(h)], after, 1, 1)
        dk_ref[:, head(h)] = dk.astype(jnp.bfloat16)
        dv = dv_part[:, head(h)] + mm(k_ref[:, head(h)], after, 1, 0)
        dv_ref[:, head(h)] = dv.astype(jnp.bfloat16)

    key_value_state(0)
    behind = n_sub - 1 - place
    greeted = jnp.minimum(place, 1) + jnp.minimum(behind, 1)
    greeted = greeted + jnp.minimum(row, 1) + jnp.minimum(n_seq - 1 - row, 1)
    pl.semaphore_wait(barrier, greeted)
    turns = (row, n_seq - 1 - row)

    @pl.loop(0, H + 2 * depth + 1)
    def _(slot):
        for scan, start in ((0, 0), (1, depth + 1)):
            now = slot - start
            in_turn(now - SUB_SKEW * place, up(scan))
            in_turn(now - SUB_SKEW * behind, down(scan))
            in_turn(now - SUB_SKEW * jnp.maximum(place, behind) - SEQ_SKEW * turns[scan], along_seq(scan))
        in_turn(slot + 1, key_value_state)
        in_turn(slot - depth, norm_and_pullback)
        in_turn(slot - 1, within_block)
        in_turn(slot - depth - 2, gradients_within)
        in_turn(slot - 2 * depth - 1, finish)

    for scan in range(2):
        leaves_seq = (has_next_row, has_prev_row)[scan]
        for kind, leaves, source in (
            (0, has_next, up_out), (1, has_prev, down_out), (2, leaves_seq, seq_out),
        ):
            @pl.when(leaves)
            def _(kind=kind, source=source, scan=scan):
                whole = source.at[scan]
                pltpu.make_async_copy(whole, whole, send_sems.at[scan, kind]).wait()


def local(n_seq, n_sub, queries, key_vectors, value_vectors, cotangent, norm_gain):
    width = H * DH
    vmem = pl.BlockSpec(memory_space=pltpu.VMEM)
    states = pltpu.VMEM((2, H, DH, DH), jnp.float32)
    wide = pltpu.VMEM((BLK, width), jnp.float32)
    return pl.pallas_call(
        functools.partial(kernel, n_seq, n_sub),
        out_shape=[jax.ShapeDtypeStruct((BLK, width), jnp.bfloat16)] * 4,
        in_specs=[vmem] * 5,
        out_specs=[vmem] * 4,
        scratch_shapes=[
            *[states] * 7,
            pltpu.VMEM((H, BLK, BLK), jnp.bfloat16),
            wide,
            pltpu.VMEM((BLK, width), jnp.bfloat16),
            wide,
            wide,
            pltpu.SemaphoreType.DMA((2, 3)),
            pltpu.SemaphoreType.DMA((2, 3, H)),
        ],
        compiler_params=pltpu.CompilerParams(
            collective_id=0, has_side_effects=True, vmem_limit_bytes=48 << 20
        ),
    )(queries, key_vectors, value_vectors, cotangent, norm_gain.reshape(1, width))


def solution(mesh):
    rows = P(("groups", "seq", "sub"), None)
    return jax.shard_map(
        functools.partial(local, mesh.shape["seq"], mesh.shape["sub"]),
        mesh=mesh,
        in_specs=(rows, rows, rows, rows, P()),
        out_specs=(rows, rows, rows, rows),
        check_vma=False,
    )
```

```python
import functools

import jax
import jax.numpy as jnp
from jax import lax
from jax.experimental import pallas as pl
from jax.experimental.pallas import tpu as pltpu
from jax.sharding import PartitionSpec as P

H = 8
DH = 128
BLK = 512
PIECES = 2
SUB_SKEW = 4
SEQ_SKEW = 2
MESH = pl.DeviceIdType.MESH


def mm(a, b, ca, cb):
    return lax.dot_general(a, b, (((ca,), (cb,)), ((), ())), preferred_element_type=jnp.float32)


def kernel(
    n_seq, n_sub, q_hbm, k_hbm, v_hbm, c_hbm, gain_hbm,
    out_ref, dq_ref, dk_ref, dv_ref,
    q_ref, k_ref, v_ref, c_ref, gain_ref,
    own, up_in, up_out, down_in, down_out, seq_in, seq_out,
    scores, attended, grad, dk_part, dv_part,
    send_sems, recv_sems, load_sems,
):
    row = lax.axis_index("seq")
    place = lax.axis_index("sub")
    has_prev, has_next = place > 0, place < n_sub - 1
    has_prev_row, has_next_row = row > 0, row < n_seq - 1
    depth = SUB_SKEW * (n_sub - 1) + SEQ_SKEW * (n_seq - 1)

    def head(h):
        return pl.ds(pl.multiple_of(h * DH, DH), DH)

    chunks, rows = H * PIECES, DH // PIECES

    def piece(c):
        return pl.ds(pl.multiple_of(c * rows, rows), rows)

    def at_sub(step):
        return {"sub": place + step}

    def at_seq(step):
        return {"seq": row + step}

    loads = [
        pltpu.make_async_copy(source, target, load_sems.at[index])
        for index, (source, target) in enumerate(
            ((k_hbm, k_ref), (v_hbm, v_ref), (q_hbm, q_ref), (c_hbm, c_ref), (gain_hbm, gain_ref))
        )
    ]
    for load in loads:
        load.start()
    barrier = pltpu.get_barrier_semaphore()
    neighbours = (
        (has_prev, at_sub(-1)), (has_next, at_sub(1)),
        (has_prev_row, at_seq(-1)), (has_next_row, at_seq(1)),
    )
    for exists, device in neighbours:
        @pl.when(exists)
        def _(device=device):
            pl.semaphore_signal(barrier, inc=1, device_id=device, device_id_type=MESH)

    first_row = (jnp.logical_not(has_prev_row), jnp.logical_not(has_next_row))
    for scan in range(2):
        for empty, buffer in (
            (jnp.logical_not(has_prev), up_in),
            (jnp.logical_not(has_next), down_in),
            (first_row[scan], seq_in),
        ):
            @pl.when(empty)
            def _(buffer=buffer, scan=scan):
                buffer[scan] = jnp.zeros((H * DH, DH), jnp.float32)

    def hop(source, landing, scan, kind, c, device):
        return pltpu.make_async_remote_copy(
            src_ref=source.at[scan, piece(c)],
            dst_ref=landing.at[scan, piece(c)],
            send_sem=send_sems.at[scan, kind],
            recv_sem=recv_sems.at[scan, kind, c],
            device_id=device,
            device_id_type=MESH,
        )

    def in_turn(c, body):
        @pl.when(jnp.logical_and(c >= 0, c < chunks))
        def _():
            body(c)

    def head_turn(c, body):
        due = jnp.logical_and(c >= 0, c < chunks)

        @pl.when(jnp.logical_and(due, lax.rem(c, PIECES) == 0))
        def _():
            body(c // PIECES)

    def link(landing, source, scan, kind, c, arrives, leaves, step, value):
        @pl.when(arrives)
        def _():
            hop(source, landing, scan, kind, c, step).wait_recv()

        source[scan, piece(c), :] = value()

        @pl.when(leaves)
        def _():
            hop(source, landing, scan, kind, c, step).start()

    def up(scan):
        def body(c):
            link(up_in, up_out, scan, 0, c, has_prev, has_next, at_sub(1),
                 lambda: up_in[scan, piece(c), :] + own[scan, piece(c), :])
        return body

    def down(scan):
        def body(c):
            link(down_in, down_out, scan, 1, c, has_next, has_prev, at_sub(-1),
                 lambda: down_in[scan, piece(c), :] + own[scan, piece(c), :])
        return body

    def along_seq(scan):
        arrives, leaves, step = (
            (has_prev_row, has_next_row, at_seq(1)),
            (has_next_row, has_prev_row, at_seq(-1)),
        )[scan]

        def body(c):
            link(seq_in, seq_out, scan, 2, c, arrives, leaves, step,
                 lambda: seq_in[scan, piece(c), :] + (up_out[scan, piece(c), :] + down_in[scan, piece(c), :]))
        return body

    def entering(scan, h):
        within = (up_in, down_in)[scan]
        return (seq_in[scan, head(h), :] + within[scan, head(h), :]).astype(jnp.bfloat16)

    def key_value_state(h):
        own[0, head(h), :] = mm(k_ref[:, head(h)], v_ref[:, head(h)], 0, 0)

    causal = lax.broadcasted_iota(jnp.int32, (BLK, BLK), 0) >= lax.broadcasted_iota(
        jnp.int32, (BLK, BLK), 1
    )

    def within_block(h):
        s = mm(q_ref[:, head(h)], k_ref[:, head(h)], 1, 1)
        s = jnp.where(causal, s, 0.0).astype(jnp.bfloat16)
        scores[h] = s
        attended[:, head(h)] = mm(s, v_ref[:, head(h)], 1, 0)

    def norm_and_pullback(h):
        q = q_ref[:, head(h)]
        att = attended[:, head(h)] + mm(q, entering(0, h), 1, 0)
        inverse = lax.rsqrt(jnp.mean(att * att, axis=-1, keepdims=True) + 1e-05)
        gain = gain_ref[:, head(h)]
        out_ref[:, head(h)] = (att * inverse * gain).astype(jnp.bfloat16)
        scaled = c_ref[:, head(h)].astype(jnp.float32) * gain
        along = jnp.mean(scaled * att, axis=-1, keepdims=True) * inverse * inverse
        g = (inverse * (scaled - att * along)).astype(jnp.bfloat16)
        grad[:, head(h)] = g
        own[1, head(h), :] = mm(q, g, 0, 0)

    def gradients_within(h):
        g = grad[:, head(h)]
        s = mm(g, v_ref[:, head(h)], 1, 1)
        s = jnp.where(causal, s, 0.0).astype(jnp.bfloat16)
        dq = mm(s, k_ref[:, head(h)], 1, 0) + mm(g, entering(0, h), 1, 1)
        dq_ref[:, head(h)] = dq.astype(jnp.bfloat16)
        dk_part[:, head(h)] = mm(s, q_ref[:, head(h)], 0, 0)
        dv_part[:, head(h)] = mm(scores[h], g, 0, 0)

    def finish(h):
        after = entering(1, h)
        dk = dk_part[:, head(h)] + mm(v_ref[:, head(h)], after, 1, 1)
        dk_ref[:, head(h)] = dk.astype(jnp.bfloat16)
        dv = dv_part[:, head(h)] + mm(k_ref[:, head(h)], after, 1, 0)
        dv_ref[:, head(h)] = dv.astype(jnp.bfloat16)

    loads[0].wait()
    loads[1].wait()
    key_value_state(0)
    for load in loads[2:]:
        load.wait()
    behind = n_sub - 1 - place
    greeted = jnp.minimum(place, 1) + jnp.minimum(behind, 1)
    greeted = greeted + jnp.minimum(row, 1) + jnp.minimum(n_seq - 1 - row, 1)
    pl.semaphore_wait(barrier, greeted)
    turns = (row, n_seq - 1 - row)

    @pl.loop(0, chunks + 2 * depth + PIECES)
    def _(slot):
        for scan, start in ((0, 0), (1, depth + PIECES)):
            now = slot - start
            in_turn(now - SUB_SKEW * place, up(scan))
            in_turn(now - SUB_SKEW * behind, down(scan))
            in_turn(now - SUB_SKEW * jnp.maximum(place, behind) - SEQ_SKEW * turns[scan], along_seq(scan))
        head_turn(slot + 1, key_value_state)
        head_turn(slot - depth - PIECES + 1, norm_and_pullback)
        head_turn(slot - 1, within_block)
        head_turn(slot - depth - PIECES - 2, gradients_within)
        head_turn(slot - 2 * depth - 2 * PIECES + 1, finish)

    for scan in range(2):
        leaves_seq = (has_next_row, has_prev_row)[scan]
        for kind, leaves, source in (
            (0, has_next, up_out), (1, has_prev, down_out), (2, leaves_seq, seq_out),
        ):
            @pl.when(leaves)
            def _(kind=kind, source=source, scan=scan):
                whole = source.at[scan]
                pltpu.make_async_copy(whole, whole, send_sems.at[scan, kind]).wait()


def local(n_seq, n_sub, queries, key_vectors, value_vectors, cotangent, norm_gain):
    width = H * DH
    vmem = pl.BlockSpec(memory_space=pltpu.VMEM)
    states = pltpu.VMEM((2, width, DH), jnp.float32)
    wide = pltpu.VMEM((BLK, width), jnp.float32)
    return pl.pallas_call(
        functools.partial(kernel, n_seq, n_sub),
        out_shape=[jax.ShapeDtypeStruct((BLK, width), jnp.bfloat16)] * 4,
        in_specs=[pl.BlockSpec(memory_space=pl.ANY)] * 5,
        out_specs=[vmem] * 4,
        scratch_shapes=[
            *[pltpu.VMEM((BLK, width), jnp.bfloat16)] * 4,
            pltpu.VMEM((1, width), jnp.float32),
            *[states] * 7,
            pltpu.VMEM((H, BLK, BLK), jnp.bfloat16),
            wide,
            pltpu.VMEM((BLK, width), jnp.bfloat16),
            wide,
            wide,
            pltpu.SemaphoreType.DMA((2, 3)),
            pltpu.SemaphoreType.DMA((2, 3, H * PIECES)),
            pltpu.SemaphoreType.DMA((5,)),
        ],
        compiler_params=pltpu.CompilerParams(
            collective_id=0, has_side_effects=True, vmem_limit_bytes=48 << 20
        ),
    )(queries, key_vectors, value_vectors, cotangent, norm_gain.reshape(1, width))


def solution(mesh):
    rows = P(("groups", "seq", "sub"), None)
    return jax.shard_map(
        functools.partial(local, mesh.shape["seq"], mesh.shape["sub"]),
        mesh=mesh,
        in_specs=(rows, rows, rows, rows, P()),
        out_specs=(rows, rows, rows, rows),
        check_vma=False,
    )
```
